32 devices in a mesh: gz: 8 (over z, x), gy: 4 (over y, core).
Axes of the slice: x: 2, y: 2, z: 4, core: 2. Of those that a mesh axis runs over, the one named last changes fastest.
Arguments:
- fields: float32 [2, 256, 256, 128], P(None, 'gz', 'gy'), may hold values from -7 to 8
- residual: float32 [2, 256, 256, 128], P(None, 'gz', 'gy'), may hold values from -14 to 14
- past_fields: float32 [20, 2, 256, 256, 128], P(None, None, 'gz', 'gy'), may hold values from -7 to 8
- past_residuals: float32 [20, 2, 256, 256, 128], P(None, None, 'gz', 'gy'), may hold values from -14 to 14
Outputs:
- new_fields: float32 [2, 256, 256, 128], P(None, 'gz', 'gy')
- summary: float32 [3], replicated
The draws below stay inside these ranges and needn't reach their ends.
All inputs are finite; a program needn't handle non-finite values.
Results may differ from the reference program's by a relative error of at most 0.0003.
Values sent between devices are 32-bit elements; how exact they have to be, the bound alone decides.
A program may use at most 192 MiB of HBM per device.

```python
import math
import jax
import jax.numpy as jnp
from jax import lax

HIST = 20
NZ = 256
NY = 256
NX = 128


TWO_PI = 2.0 * math.pi


def low_modes(key, count):
    amplitude = jax.random.uniform(jax.random.fold_in(key, 1), (count, 4), jnp.float32, -1.0, 1.0)
    phase = jax.random.uniform(jax.random.fold_in(key, 2), (count, 4), jnp.float32, 0.0, TWO_PI)
    height = (lax.iota(jnp.int32, NZ).astype(jnp.float32) / NZ)[None, :, None]
    width = (lax.iota(jnp.int32, NY).astype(jnp.float32) / NY)[None, None, :]
    total = amplitude[:, 0, None, None] * jnp.sin(TWO_PI * height + phase[:, 0, None, None])
    total = total + amplitude[:, 1, None, None] * jnp.sin(TWO_PI * width + phase[:, 1, None, None])
    total = total + amplitude[:, 2, None, None] * jnp.sin(TWO_PI * (height + width) + phase[:, 2, None, None])
    total = total + amplitude[:, 3, None, None] * jnp.sin(TWO_PI * (2.0 * height - width) + phase[:, 3, None, None])
    return total


def high_modes(key):
    phase = jax.random.uniform(jax.random.fold_in(key, 1), (5,), jnp.float32, 0.0, TWO_PI)
    height = lax.iota(jnp.int32, NZ).astype(jnp.float32) / NZ
    width = lax.iota(jnp.int32, NY).astype(jnp.float32) / NY
    line = lax.iota(jnp.int32, NX).astype(jnp.float32) / NX
    third_z = jnp.sin(TWO_PI * 3.0 * height + phase[0])[:, None, None] * jnp.cos(TWO_PI * line + phase[1])[None, None, :]
    fourth_y = jnp.sin(TWO_PI * 4.0 * width + phase[2])[None, :, None] * jnp.cos(TWO_PI * 2.0 * line + phase[3])[None, None, :]
    slanted = jnp.sin(TWO_PI * (5.0 * height[:, None] + 3.0 * width[None, :]) + phase[4])[:, :, None]
    pattern = 1.5 * third_z + 1.0 * fourth_y + 0.8 * slanted
    species_sign = jnp.array([1.0, -0.8], jnp.float32)
    return species_sign[:, None, None, None] * pattern[None, :, :, :]


def current_residual(key):
    source = jax.random.fold_in(key, 101)
    spread = jnp.exp(jax.random.uniform(jax.random.fold_in(source, 1), (NZ,), jnp.float32, -0.7, 0.7))
    rough = jnp.clip(jax.random.normal(jax.random.fold_in(source, 2), (2, NZ, NY, NX), jnp.float32), -2.5, 2.5)
    offset = jax.random.uniform(jax.random.fold_in(source, 3), (NZ, NY), jnp.float32, -0.8, 0.8)
    broad = 1.2 * low_modes(jax.random.fold_in(source, 4), 1)[0]
    sharp = high_modes(jax.random.fold_in(source, 5))
    total = rough * spread[None, :, None, None] + (offset + broad)[None, :, :, None] + sharp
    return jnp.clip(total, -14.0, 14.0)


def draw_residual(key, part):
    return current_residual(key)


def draw_past_residuals(key, part):
    current = current_residual(key)
    source = jax.random.fold_in(key, 202)
    decay = jax.random.uniform(jax.random.fold_in(source, 1), (HIST,), jnp.float32, 0.3, 0.95)
    weight = jnp.exp(jax.random.uniform(jax.random.fold_in(source, 2), (HIST,), jnp.float32, math.log(0.4), 0.0))
    phase = jax.random.uniform(jax.random.fold_in(source, 3), (HIST, 2), jnp.float32, 0.0, TWO_PI)
    bumps = jax.random.uniform(jax.random.fold_in(source, 4), (HIST, NZ), jnp.float32, -0.15, 0.15)
    broad = low_modes(jax.random.fold_in(source, 5), HIST)
    height = lax.iota(jnp.int32, NZ).astype(jnp.float32) / NZ
    width = lax.iota(jnp.int32, NY).astype(jnp.float32) / NY
    shared = jnp.zeros((), jnp.float32)
    own_share = 1.0
    shared_share = 0.0

    def one_iterate(index):
        tilt = 0.6 * jnp.sin(TWO_PI * height + phase[index, 0])[:, None] + 0.3 * jnp.sin(TWO_PI * width + phase[index, 1])[None, :] + bumps[index][:, None]
        envelope = jnp.exp(tilt)
        rough = jnp.clip(jax.random.normal(jax.random.fold_in(source, 1000 + index), (2, NZ, NY, NX), jnp.float32), -2.5, 2.5)
        sharp = 0.6 * high_modes(jax.random.fold_in(source, 2000 + index))
        noise = (own_share * rough + shared_share * shared + 0.5 * broad[index][None, :, :, None]) * envelope[None, :, :, None] + sharp
        return jnp.clip(decay[index] * current + weight[index] * noise, -14.0, 14.0)
    return lax.map(one_iterate, lax.iota(jnp.int32, HIST))


def species_field(key):
    spread = 1.5
    rough = jnp.clip(jax.random.normal(key, (2, NZ, NY, NX), jnp.float32), -3.0, 3.0)
    level = jnp.array([2.0, -1.0], jnp.float32)
    return spread * rough + level[:, None, None, None]


def draw_fields(key, part):
    return species_field(jax.random.fold_in(key, 303))


def draw_past_fields(key, part):
    source = jax.random.fold_in(key, 404)

    def one_iterate(index):
        return species_field(jax.random.fold_in(source, index))
    return lax.map(one_iterate, lax.iota(jnp.int32, HIST))


def setup_inputs(seed: int = 0) -> dict:
    streams_of = jax.random.split(jax.random.key(seed), 5)
    fields = draw_fields(jax.random.fold_in(streams_of[4], 71), 0)
    residual = draw_residual(jax.random.fold_in(streams_of[4], 71), 0)
    past_fields = draw_past_fields(jax.random.fold_in(streams_of[4], 71), 0)
    past_residuals = draw_past_residuals(jax.random.fold_in(streams_of[4], 71), 0)
    return {"fields": fields, "residual": residual, "past_fields": past_fields, "past_residuals": past_residuals}


CHI_N = 20.0
RIDGE = 0.01
STEP_LOCAL = 0.1
EXACT = lax.Precision.HIGHEST

def kernel_table(length):
    decay_len = length / 4.0
    row_index = lax.iota(jnp.int32, length)[:, None]
    col_index = lax.iota(jnp.int32, length)[None, :]
    lag = jnp.mod(row_index - col_index, length).astype(jnp.float32)
    offsets = lax.iota(jnp.int32, length).astype(jnp.float32)
    normalizer = jnp.sum(jnp.cosh((0.5 * length - offsets) / decay_len))
    return jnp.cosh((0.5 * length - lag) / decay_len) / normalizer

def reference(fields, residual, past_fields, past_residuals):
    history = past_residuals.shape[0]

    def gram_step(plane, carry):
        gram_acc, intersect_acc = carry
        current = lax.dynamic_slice_in_dim(residual, plane, 1, 1).reshape(-1)
        earlier = lax.dynamic_slice_in_dim(past_residuals, plane, 1, 2).reshape(history, -1)
        deltas = current[None, :] - earlier
        gram_acc = gram_acc + jnp.dot(deltas.astype(jnp.float32), deltas.T.astype(jnp.float32), precision=EXACT, preferred_element_type=jnp.float32)
        intersect_acc = intersect_acc + jnp.dot(deltas.astype(jnp.float32), current.astype(jnp.float32), precision=EXACT, preferred_element_type=jnp.float32)
        return (gram_acc, intersect_acc)
    start = (jnp.zeros((history, history), jnp.float32), jnp.zeros((history,), jnp.float32))
    gram_matrix, intersect = lax.fori_loop(0, NZ, gram_step, start)
    diagonal_shift = RIDGE * jnp.trace(gram_matrix) / history + 1.0
    system = gram_matrix + diagonal_shift * jnp.eye(history, dtype=jnp.float32)
    factor = jnp.linalg.cholesky(system)
    forward = lax.linalg.triangular_solve(factor, intersect[:, None], left_side=True, lower=True)
    coeffs = lax.linalg.triangular_solve(factor, forward, left_side=True, lower=True, transpose_a=True)[:, 0]
    remain_weight = 1.0 - jnp.sum(coeffs)
    field_mixed = remain_weight * fields + jnp.dot(coeffs.astype(jnp.float32), past_fields.reshape(history, -1).astype(jnp.float32), precision=EXACT, preferred_element_type=jnp.float32).reshape(fields.shape)
    residual_mixed = remain_weight * residual + jnp.dot(coeffs.astype(jnp.float32), past_residuals.reshape(history, -1).astype(jnp.float32), precision=EXACT, preferred_element_type=jnp.float32).reshape(residual.shape)
    kernel_z = kernel_table(NZ)
    kernel_y = kernel_table(NY)
    smoothed = jnp.einsum('ab,sbyx->sayx', kernel_z, residual_mixed, precision=EXACT)
    smoothed = jnp.einsum('ab,szbx->szax', kernel_y, smoothed, precision=EXACT)
    new_fields = field_mixed + STEP_LOCAL * residual_mixed + smoothed
    split_field = new_fields[0] - new_fields[1]
    sum_field = new_fields[0] + new_fields[1]
    energy = jnp.mean(split_field * split_field / (4.0 * CHI_N) - 0.5 * sum_field)
    relative = jnp.sqrt(jnp.sum(residual * residual) / (jnp.sum(fields * fields) + 1.0))
    largest = jnp.max(jnp.abs(residual_mixed))
    summary = jnp.stack([energy, relative, largest])
    return (new_fields, summary)
```

```python
import functools
import math

import jax
import jax.numpy as jnp
import numpy as np
from jax import lax
from jax.experimental import pallas as pl
from jax.experimental.pallas import tpu as pltpu
from jax.sharding import PartitionSpec as P

CHI_N = 20.0
RIDGE = 0.01
STEP_LOCAL = 0.1
EXACT = lax.Precision.HIGHEST
NT = (((1,), (1,)), ((), ()))


def params(count):
    return pltpu.CompilerParams(
        dimension_semantics=("arbitrary",) * count, vmem_limit_bytes=56 * 1024 * 1024
    )


def gram_kernel(history, past_ref, res_ref, field_ref, out_ref, high, low, acc, square):
    step = pl.program_id(0)

    @pl.when(step == 0)
    def _():
        acc[...] = jnp.zeros_like(acc)
        square[...] = jnp.zeros_like(square)

    rows = res_ref.shape[0]
    used = 8 * history
    size = high.shape[0]
    for g in range(rows // 8):
        part = pl.ds(8 * g, 8)
        lanes = pl.ds(128 * g, 128)
        current = res_ref[part, :]
        delta = (current[None] - past_ref[:, part, :]).reshape(used, 128)
        tail = jnp.concatenate([current, jnp.zeros((size - used - 8, 128), jnp.float32)], axis=0)
        for first, value in ((0, delta), (used, tail)):
            head = value.astype(jnp.bfloat16)
            rest = (value - head.astype(jnp.float32)).astype(jnp.bfloat16)
            high[pl.ds(first, value.shape[0]), lanes] = head
            low[pl.ds(first, value.shape[0]), lanes] = rest
    hi, lo = high[...], low[...]
    acc[0] += lax.dot_general(hi, hi, NT, preferred_element_type=jnp.float32)
    acc[1] += lax.dot_general(hi, lo, NT, preferred_element_type=jnp.float32)
    field = field_ref[...]
    square[...] += jnp.sum((field * field).reshape(rows // 8, 8, 128), axis=0)

    @pl.when(step == pl.num_programs(0) - 1)
    def _():
        same = lax.broadcasted_iota(jnp.int32, (size, size), 0) % 8 == (
            lax.broadcasted_iota(jnp.int32, (size, size), 1) % 8
        )
        pick_rows = (
            lax.broadcasted_iota(jnp.int32, (24, size), 1) // 8
            == lax.broadcasted_iota(jnp.int32, (24, size), 0)
        ).astype(jnp.float32)
        pick_cols = (
            lax.broadcasted_iota(jnp.int32, (128, size), 1) // 8
            == lax.broadcasted_iota(jnp.int32, (128, size), 0)
        ).astype(jnp.float32)

        def fold(a, b, value):
            inner = jnp.dot(a, jnp.where(same, value, 0.0), precision=EXACT, preferred_element_type=jnp.float32)
            return lax.dot_general(inner, b, NT, precision=EXACT, preferred_element_type=jnp.float32)

        cross = acc[1]
        out_ref[pl.ds(0, 24), :] = fold(pick_rows, pick_cols, acc[0] + cross + cross.T)
        out_ref[pl.ds(24, 8), :] = square[...]


def solve(history, parts_ref, coeff_ref, stats_ref):
    total = parts_ref[0]
    for k in range(1, parts_ref.shape[0]):
        total = total + parts_ref[k]
    matrix = total[0:24]
    field_square = jnp.sum(jnp.sum(total[24:32], axis=0, keepdims=True), axis=1, keepdims=True)
    residual_square = matrix[history : history + 1, history : history + 1]
    row = lax.broadcasted_iota(jnp.int32, (24, 128), 0)
    col = lax.broadcasted_iota(jnp.int32, (24, 128), 1)
    diagonal = (row == col) & (row < history)
    trace = jnp.sum(
        jnp.sum(jnp.where(diagonal, matrix, 0.0), axis=0, keepdims=True), axis=1, keepdims=True
    )
    shift = RIDGE * trace / history + 1.0
    matrix = jnp.where(row < history, matrix + jnp.where(diagonal, shift, 0.0), 0.0)
    for k in range(history):
        pivot = matrix[k : k + 1, :]
        scaled = pivot / matrix[k : k + 1, k : k + 1]
        column = matrix[:, k : k + 1]
        matrix = jnp.where(row == k, scaled, matrix - column * scaled)
    coeffs = jnp.broadcast_to(matrix[:, history : history + 1], (24, 128))
    remain = 1.0 - jnp.sum(coeffs, axis=0, keepdims=True)
    coeff_ref[...] = jnp.where(row == history, remain, coeffs)
    relative = jnp.sqrt(residual_square / (field_square + 1.0))
    stats_ref[pl.ds(0, 8), :] = jnp.zeros((8, 128), jnp.float32)
    stats_ref[pl.ds(8, 8), :] = jnp.broadcast_to(relative, (8, 128))


def mix_kernel(
    history, decay, parts_ref, pf_ref, pr_ref, field_ref, res_ref, base_ref, mixed_ref, ends_ref, stats_ref, coeff
):
    species, step = pl.program_id(0), pl.program_id(1)

    @pl.when((species == 0) & (step == 0))
    def _():
        solve(history, parts_ref, coeff, stats_ref)

    @pl.when(step == 0)
    def _():
        ends_ref[...] = jnp.zeros_like(ends_ref)

    planes, rows = res_ref.shape[1], res_ref.shape[2]
    peak = stats_ref[pl.ds(0, 8), :]
    weights = [coeff[pl.ds(i, 1), :] for i in range(history + 1)]
    for z in range(planes):
        place = jnp.full((1, 128), step * planes + z, jnp.int32).astype(jnp.float32)
        back = jnp.exp(-place * decay)
        for g in range(rows // 8):
            part = pl.ds(8 * g, 8)
            mixed = weights[history] * res_ref[0, z, part, :]
            field = weights[history] * field_ref[0, z, part, :]
            for i in range(history):
                mixed = mixed + weights[i] * pr_ref[i, 0, z, part, :]
                field = field + weights[i] * pf_ref[i, 0, z, part, :]
            mixed_ref[0, z, part, :] = mixed
            base_ref[0, z, part, :] = field + STEP_LOCAL * mixed
            peak = jnp.maximum(peak, jnp.abs(mixed))
            ends_ref[0, 0, part, :] = ends_ref[0, 0, part, :] * math.exp(-decay) + mixed
            ends_ref[0, 1, part, :] += back * mixed
    stats_ref[pl.ds(0, 8), :] = peak


def smooth_kernel(decay, weight_ref, ends_ref, taps_ref, mixed_ref, base_ref, out_ref, tops_ref, work):
    planes, rows = mixed_ref.shape[1], mixed_ref.shape[2]
    ratio = math.exp(-decay)
    blocks = ends_ref.shape[0]

    def carried(side):
        total = weight_ref[side, 0] * ends_ref[0, 0, side]
        for k in range(1, blocks):
            total = total + weight_ref[side, k] * ends_ref[k, 0, side]
        return total

    carry = carried(0)
    for z in range(planes):
        carry = carry * ratio + mixed_ref[0, z]
        work[z] = carry
    carry = carried(1)
    taps = taps_ref[...]
    for z in range(planes - 1, -1, -1):
        plane = work[z] + ratio * carry
        carry = carry * ratio + mixed_ref[0, z]
        result = jnp.dot(taps, plane, precision=EXACT, preferred_element_type=jnp.float32)
        out_ref[0, z] = base_ref[0, z] + result[0:rows]
        tops_ref[0, 0, pl.ds(z, 1), :] = result[rows : rows + 1]
        tops_ref[0, 1, pl.ds(z, 1), :] = result[rows + 1 : rows + 2]


def finish_kernel(decay, weight_ref, tops_ref, part_ref, out_ref, energy_ref):
    step = pl.program_id(0)

    @pl.when(step == 0)
    def _():
        energy_ref[...] = jnp.zeros_like(energy_ref)

    planes, rows = part_ref.shape[1], part_ref.shape[2]
    blocks = tops_ref.shape[0]
    place = lax.broadcasted_iota(jnp.int32, (rows, 128), 0).astype(jnp.float32)
    down = jnp.exp(-(place + 1.0) * decay)
    up = jnp.exp(-(rows - place) * decay)
    carry = []
    for s in range(2):
        pair = []
        for side in range(2):
            total = weight_ref[side, 0] * tops_ref[0, s, side]
            for k in range(1, blocks):
                total = total + weight_ref[side, k] * tops_ref[k, s, side]
            pair.append(total)
        carry.append(pair)
    energy = energy_ref[...]
    for z in range(planes):
        new = []
        for s in range(2):
            value = (
                part_ref[s, z]
                + down * carry[s][0][z : z + 1, :]
                + up * carry[s][1][z : z + 1, :]
            )
            out_ref[s, z] = value
            new.append(value)
        split = new[0] - new[1]
        term = split * split / (4.0 * CHI_N) - 0.5 * (new[0] + new[1])
        energy = energy + jnp.sum(term.reshape(rows // 8, 8, 128), axis=0)
    energy_ref[...] = energy


def carry_weights(axis, cells, total):
    blocks = lax.axis_size(axis)
    me = lax.axis_index(axis)
    step = 4.0 * cells / total
    other = lax.iota(jnp.int32, blocks)
    scale = 1.0 / (1.0 - math.exp(-4.0))
    below = jnp.mod(me - other - 1, blocks).astype(jnp.float32)
    above = jnp.mod(other - me - 1, blocks).astype(jnp.float32)
    return scale * jnp.exp(-step * jnp.stack([below, above]))


def unit(decay):
    ratio = math.exp(-decay)
    return (1.0 - ratio) / (1.0 + ratio)


def shards(fields, residual, past_fields, past_residuals):
    history = past_residuals.shape[0]
    species, height_cells, width_cells, line_cells = residual.shape
    height_total = height_cells * lax.axis_size("gz")
    width_total = width_cells * lax.axis_size("gy")
    cell_total = height_total * width_total * line_cells
    decay_z, decay_y = 4.0 / height_total, 4.0 / width_total
    lines = species * height_cells * width_cells
    f32 = jnp.float32

    rows = min(256, lines)
    size = -(-(history + 1) // 2) * 16
    local = pl.pallas_call(
        functools.partial(gram_kernel, history),
        grid=(lines // rows,),
        in_specs=[
            pl.BlockSpec((history, rows, line_cells), lambda i: (0, i, 0)),
            pl.BlockSpec((rows, line_cells), lambda i: (i, 0)),
            pl.BlockSpec((rows, line_cells), lambda i: (i, 0)),
        ],
        out_specs=pl.BlockSpec((32, 128), lambda i: (0, 0)),
        out_shape=jax.ShapeDtypeStruct((32, 128), f32),
        scratch_shapes=[
            pltpu.VMEM((size, rows // 8 * 128), jnp.bfloat16),
            pltpu.VMEM((size, rows // 8 * 128), jnp.bfloat16),
            pltpu.VMEM((2, size, size), f32),
            pltpu.VMEM((8, 128), f32),
        ],
        compiler_params=params(1),
        name="gram",
    )(
        past_residuals.reshape(history, lines, line_cells),
        residual.reshape(lines, line_cells),
        fields.reshape(lines, line_cells),
    )
    parts = lax.all_gather(local, ("gz", "gy"), axis=0, tiled=False)

    planes = 2 if height_cells % 2 == 0 else 1
    slab = (1, planes, width_cells, line_cells)
    slab_map = lambda s, z: (s, z, 0, 0)
    grid_shape = jax.ShapeDtypeStruct(residual.shape, f32)
    base, mixed, ends, stats = pl.pallas_call(
        functools.partial(mix_kernel, history, decay_z),
        grid=(species, height_cells // planes),
        in_specs=[
            pl.BlockSpec(parts.shape, lambda s, z: (0, 0, 0)),
            pl.BlockSpec((history, *slab), lambda s, z: (0, s, z, 0, 0)),
            pl.BlockSpec((history, *slab), lambda s, z: (0, s, z, 0, 0)),
            pl.BlockSpec(slab, slab_map),
            pl.BlockSpec(slab, slab_map),
        ],
        out_specs=[
            pl.BlockSpec(slab, slab_map),
            pl.BlockSpec(slab, slab_map),
            pl.BlockSpec((1, 2, width_cells, line_cells), lambda s, z: (s, 0, 0, 0)),
            pl.BlockSpec((16, 128), lambda s, z: (0, 0)),
        ],
        out_shape=[
            grid_shape,
            grid_shape,
            jax.ShapeDtypeStruct((species, 2, width_cells, line_cells), f32),
            jax.ShapeDtypeStruct((16, 128), f32),
        ],
        scratch_shapes=[pltpu.VMEM((24, 128), f32)],
        compiler_params=params(2),
        name="mix",
    )(parts, past_fields, past_residuals, fields, residual)
    every_end = lax.all_gather(ends, "gz", axis=0, tiled=False)

    ratio = math.exp(-decay_y)
    offset = np.arange(width_cells)
    taps = np.zeros((width_cells + 8, width_cells))
    taps[:width_cells] = ratio ** np.abs(offset[:, None] - offset[None, :])
    taps[width_cells] = ratio ** (width_cells - 1 - offset)
    taps[width_cells + 1] = ratio ** offset
    taps = jnp.asarray(taps * unit(decay_y) * unit(decay_z), f32)
    whole = pl.BlockSpec((1, height_cells, width_cells, line_cells), lambda s: (s, 0, 0, 0))
    partial, tops = pl.pallas_call(
        functools.partial(smooth_kernel, decay_z),
        grid=(species,),
        in_specs=[
            pl.BlockSpec(memory_space=pltpu.SMEM),
            pl.BlockSpec(
                (every_end.shape[0], 1, 2, width_cells, line_cells), lambda s: (0, s, 0, 0, 0)
            ),
            pl.BlockSpec(taps.shape, lambda s: (0, 0)),
            whole,
            whole,
        ],
        out_specs=[
            whole,
            pl.BlockSpec((1, 2, height_cells, line_cells), lambda s: (s, 0, 0, 0)),
        ],
        out_shape=[
            grid_shape,
            jax.ShapeDtypeStruct((species, 2, height_cells, line_cells), f32),
        ],
        scratch_shapes=[pltpu.VMEM((height_cells, width_cells, line_cells), f32)],
        compiler_params=params(1),
        name="smooth",
    )(carry_weights("gz", height_cells, height_total), every_end, taps, mixed, base)
    every_top = lax.all_gather(tops, "gy", axis=0, tiled=False)

    chunk = 8
    both = pl.BlockSpec((species, chunk, width_cells, line_cells), lambda z: (0, z, 0, 0))
    new_fields, energy = pl.pallas_call(
        functools.partial(finish_kernel, decay_y),
        grid=(height_cells // chunk,),
        in_specs=[
            pl.BlockSpec(memory_space=pltpu.SMEM),
            pl.BlockSpec(
                (every_top.shape[0], species, 2, chunk, line_cells), lambda z: (0, 0, 0, z, 0)
            ),
            both,
        ],
        out_specs=[both, pl.BlockSpec((8, 128), lambda z: (0, 0))],
        out_shape=[grid_shape, jax.ShapeDtypeStruct((8, 128), f32)],
        compiler_params=params(1),
        name="finish",
    )(carry_weights("gy", width_cells, width_total), every_top, partial)

    pairs = lax.all_gather(
        jnp.concatenate([energy, stats], axis=0), ("gz", "gy"), axis=0, tiled=False
    )
    summary = jnp.stack(
        [jnp.sum(pairs[:, 0:8]) / cell_total, pairs[0, 16, 0], jnp.max(pairs[:, 8:16])]
    )
    return (new_fields, summary)


def solution(mesh):
    placed = (
        P(None, "gz", "gy", None),
        P(None, "gz", "gy", None),
        P(None, None, "gz", "gy", None),
        P(None, None, "gz", "gy", None),
    )
    return jax.shard_map(
        shards,
        mesh=mesh,
        in_specs=placed,
        out_specs=(P(None, "gz", "gy", None), P()),
        check_vma=False,
    )
```
